768 devices in a mesh: ctx: 12 (over z), ch: 64 (over x, y, core).
Axes of the slice: x: 4, y: 8, z: 12, core: 2. Of those that a mesh axis runs over, the one named last changes fastest.
Arguments:
- stream: bfloat16 [1536, 8192], P('ctx', 'ch'), may hold values from -6 to 6
- in_weight: bfloat16 [8192, 3, 8192], P(None, None, 'ch'), may hold values from -0.0625 to 0.0625
- pole_rate: float32 [8192, 16], P('ch'), may hold values from 0.00032552084 to 0.05
- residue: float32 [8192, 16], P('ch'), may hold values from -1.5 to 1.5
- skip_gain: float32 [8192], P('ch'), may hold values from -4 to 4
- doc_lengths: int32 [8], replicated, may hold values from 1 to 768, 1536 in all
Outputs:
- mixed: bfloat16 [1536, 8192], P('ctx', 'ch')
The draws below stay inside these ranges and needn't reach their ends.
Inputs may be any that keep to these rules, and one draw needn't show every extreme that they name: `doc_lengths`: the 8 documents lie end to end and cover the row: the lengths sum to 1536, and the longest has exactly 1536 // 2 tokens.
All inputs are finite; a program needn't handle non-finite values.
Results may differ from the reference program's by a relative error of at most 0.003.
Values may be sent and summed in bfloat16 or wider, within the bound.
A program may use at most 64 MiB of HBM per device.

```python
import math
import jax
import jax.numpy as jnp
import numpy as np
from jax import lax

D = 8192
MODES = 16
DOCS = 8
TOKENS = 1536


def levels(stream_key, extent, cuts, least, high):
    def one(axis_at, shards_of):
        draws = jax.random.uniform(jax.random.fold_in(jax.random.fold_in(stream_key, 6), axis_at), (shards_of,), jnp.float32, least / len(cuts), high / len(cuts))
        return jnp.repeat(jnp.exp(draws), extent[axis_at] // shards_of).reshape((-1,) + (1,) * (len(extent) - axis_at - 1))

    loudness = one(*cuts[0])
    for cut in cuts[1:]:
        loudness = loudness * one(*cut)
    return loudness


def profile(count, total, reach, slope):
    portions = [(1 << 20) // math.isqrt(rank ** slope) + 1 for rank in range(2, count + 1)]
    rest, counts = total - reach - (count - 1), [1] * (count - 1)
    while rest > 0:
        movable = [i for i in range(count - 1) if counts[i] < reach]
        mass, budget = sum([portions[i] for i in movable]), rest
        for i in movable:
            more = min(reach - counts[i], max(1, budget * portions[i] // mass), rest)
            counts[i] = counts[i] + more
            rest = rest - more
    return np.array([reach] + counts)


def uneven_parts(rng, number_of, total, most, lean):
    if number_of == 2:
        one = jax.random.randint(rng, (), max(1, total - most), min(most, total - 1) + 1)
        return jnp.stack([one, total - one])
    sizes = jnp.asarray(profile(number_of, total, most, lean), jnp.int32)
    pairs = (number_of - 1) // 2
    giver, taker = sizes[1:1 + 2 * pairs:2], sizes[2:2 + 2 * pairs:2]
    margin = jnp.minimum(giver - 1, most - taker)
    shifted = jax.random.randint(jax.random.fold_in(rng, 1), (pairs,), 0, 1 << 20) % (margin + 1)
    sizes = sizes.at[1:1 + 2 * pairs:2].set(giver - shifted).at[2:2 + 2 * pairs:2].set(taker + shifted)
    return sizes[jax.random.permutation(jax.random.fold_in(rng, 2), number_of)]


def normal_values(own_key, extent, deviation, most, split=(), kind=jnp.bfloat16):
    level = levels(own_key, extent, split, -0.22, 0.18) if split else 1.0
    array = jax.random.normal(own_key, extent, jnp.float32) * deviation * level
    return jnp.minimum(jnp.maximum(array, -most), most).astype(kind)


def setup_inputs(seed: int = 0) -> dict:
    key_list = jax.random.split(jax.random.key(seed), 7)
    stream = normal_values(key_list[0], (TOKENS, D), 1.0, 6.0, ((0, 12), (1, 64)))
    in_weight = normal_values(key_list[1], (D, 3, D), D ** -0.5, 0.0625, ((2, 64),))
    pole_rate = jnp.clip(jnp.exp(math.log(0.05) - 5.034352 * jax.random.uniform(key_list[2], (D, MODES), jnp.float32) ** levels(key_list[2], (D, MODES), ((0, 64),), -0.2, 0.2)), 0.00032552084, 0.05)
    residue = normal_values(key_list[3], (D, MODES), MODES ** -0.5, 1.5, ((0, 64),), jnp.float32)
    skip_gain = normal_values(key_list[4], (D,), 1.0, 4.0, ((0, 64),), jnp.float32)
    doc_lengths = uneven_parts(key_list[5], DOCS, TOKENS, TOKENS // 2, 2).astype(jnp.int32)
    return {"stream": stream, "in_weight": in_weight, "pole_rate": pole_rate, "residue": residue, "skip_gain": skip_gain, "doc_lengths": doc_lengths}


def reference(stream, in_weight, pole_rate, residue, skip_gain, doc_lengths):
    floats = stream.astype(jnp.float32)
    rowscale = lax.rsqrt(lax.optimization_barrier(jnp.sum(floats * floats, axis=1)) / D + 1e-06)
    proj = jnp.dot(stream, in_weight.reshape(D, 3 * D), preferred_element_type=jnp.float32)
    proj = proj * rowscale[:, None]
    outer = proj[:, :D]
    inner = proj[:, D:2 * D]
    values = proj[:, 2 * D:]
    driven = inner * values
    lam = jnp.exp(-pole_rate)
    mix = residue * jnp.sqrt(-jnp.expm1(-2.0 * pole_rate))
    starts = (jnp.cumsum(doc_lengths) - doc_lengths).astype(jnp.int32)
    position = jnp.arange(TOKENS, dtype=jnp.int32)
    is_start = jnp.any(position[:, None] == starts[None, :], axis=1)
    keep = jnp.where(is_start, 0.0, 1.0).astype(jnp.float32)

    def advance(state, inputs):
        drive_row, keep_row = inputs
        state = lam * state * keep_row + drive_row[:, None]
        return (state, lax.optimization_barrier(jnp.sum(mix * state, axis=1)))
    start_state = jnp.zeros((D, MODES), jnp.float32)
    _, filtered = lax.scan(advance, start_state, (driven, keep))
    return (outer * (filtered + skip_gain[None, :] * driven)).astype(jnp.bfloat16)
```

```python
import functools

import jax
import jax.numpy as jnp
from jax import lax
from jax.experimental import pallas as pl
from jax.experimental.pallas import tpu as pltpu
from jax.sharding import PartitionSpec as P

MESH = pl.DeviceIdType.MESH
NX, NY = 4, 8
ROWS = 128
LOCAL = 128
MODES = 16
ROWS_A = 64
ROWS_B = ROWS - ROWS_A
REACH = 6
F32 = jnp.float32


def kernel(
    n_ctx, width,
    stream, w3, pole_h, resid_h, skip_h, docs_h, out,
    ga, gb, w, acc, sq, drv, y8, sw, lk, t2, pole, resid, skip, mine, got, gains, docs,
    w_sem, prm_sem, own_sem,
    a1_send, a1_recv, b1_send, b1_recv,
    ar_send, ar_recv, al_send, al_recv,
    br_send, br_recv, bl_send, bl_recv,
    as_send, as_recv, bs_send, bs_recv,
    z_send, z_recv,
):
    block = lax.axis_index("ctx")
    ch = lax.axis_index("ch")
    core = lax.rem(ch, 2)
    y = lax.rem(ch // 2, NY)
    x = ch // (2 * NY)

    def at(px, py, pc):
        return {"ch": (px * NY + py) * 2 + pc}

    def along_x(k):
        return lax.rem(x + (k + NX), NX)

    def along_y(k):
        return lax.rem(y + (k + NY), NY)

    def along_z(k):
        return lax.rem(block + (k + n_ctx), n_ctx)

    def remote(src, dst, send, recv, device):
        return pltpu.make_async_remote_copy(
            src_ref=src, dst_ref=dst, send_sem=send, recv_sem=recv,
            device_id=device, device_id_type=MESH,
        )

    parts = [
        pltpu.make_async_copy(w3.at[j], w.at[:, pl.ds(j * LOCAL, LOCAL)], w_sem.at[j])
        for j in range(3)
    ]
    params = [
        pltpu.make_async_copy(src, dst, prm_sem.at[i])
        for i, (src, dst) in enumerate(
            ((pole_h, pole), (resid_h, resid), (skip_h, skip), (docs_h, docs))
        )
    ]
    own_a = pltpu.make_async_copy(stream.at[pl.ds(0, ROWS_A)], ga.at[y, core, x], own_sem.at[0])
    own_b = pltpu.make_async_copy(stream.at[pl.ds(ROWS_A, ROWS_B)], gb.at[x, core, y], own_sem.at[1])
    own_a.start()
    own_b.start()
    for p in params:
        p.start()

    sibling = at(x, y, 1 - core)
    z_offsets = sorted({k % n_ctx for d in range(1, REACH + 1) for k in (d, -d)})
    friends = [sibling]
    friends += [at(along_x(k), y, core) for k in range(1, NX)]
    friends += [at(x, along_y(k), core) for k in range(1, NY)]
    friends += [{"ctx": along_z(k)} for k in z_offsets]
    barrier = pltpu.get_barrier_semaphore()
    for friend in friends:
        pl.semaphore_signal(barrier, inc=1, device_id=friend, device_id_type=MESH)
    for p in parts:
        p.start()
    pl.semaphore_wait(barrier, len(friends))

    a1 = [
        remote(stream.at[pl.ds(0, ROWS_A)], ga.at[y, core, x],
               a1_send.at[k - 1], a1_recv.at[k - 1], at(along_x(k), y, core))
        for k in range(1, NX)
    ]
    b1 = {
        k: remote(stream.at[pl.ds(ROWS_A, ROWS_B)], gb.at[x, core, y],
                  b1_send.at[k - 1], b1_recv.at[k - 1], at(x, along_y(k), core))
        for k in range(1, NY)
    }
    for c in a1:
        c.start()
    for k in (1, 7, 2, 6, 3, 5, 4):
        b1[k].start()

    sent = []

    def go(copy):
        copy.start()
        sent.append(copy)

    def a_right(step, lo, hi, group):
        ref = ga.at[group, core, pl.ds(lo, hi - lo)]
        return remote(ref, ref, ar_send.at[step], ar_recv.at[step], at(x, along_y(1), core))

    def a_left(step, lo, hi, group):
        ref = ga.at[group, core, pl.ds(lo, hi - lo)]
        return remote(ref, ref, al_send.at[step], al_recv.at[step], at(x, along_y(-1), core))

    def b_right(step, lo, hi, group):
        ref = gb.at[group, core, pl.ds(lo, hi - lo)]
        return remote(ref, ref, br_send.at[step], br_recv.at[step], at(along_x(1), y, core))

    def b_left(step, lo, hi, group):
        ref = gb.at[group, core, pl.ds(lo, hi - lo)]
        return remote(ref, ref, bl_send.at[step], bl_recv.at[step], at(along_x(-1), y, core))

    def a_sib(k, group, c):
        ref = ga.at[group, c]
        return remote(ref, ref, as_send.at[k], as_recv.at[k], sibling)

    def b_sib(k, group, c):
        ref = gb.at[group, c]
        return remote(ref, ref, bs_send.at[k], bs_recv.at[k], sibling)

    def add_group(buf, group, count, base, stride, lo, rows):
        def body(i, carry):
            total, squares = carry
            lhs = jnp.concatenate([buf[group, 0, i], buf[group, 1, i]], axis=1)
            first = pl.multiple_of(base + i * stride, 2 * LOCAL)
            total = total + jnp.dot(lhs, w[pl.ds(first, 2 * LOCAL), :], preferred_element_type=F32)
            f = lhs.astype(F32)
            f = f * f
            return total, squares + (f[:, :LOCAL] + f[:, LOCAL:])

        where = pl.ds(lo, rows)
        total, squares = lax.fori_loop(0, count, body, (acc[where, :], sq[where, :]))
        acc[where, :] = total
        sq[where, :] = squares

    def dots_a(k):
        group = along_y(k)
        add_group(ga, group, NX, group * (2 * LOCAL), NY * 2 * LOCAL, 0, ROWS_A)

    def dots_b(k):
        group = along_x(k)
        add_group(gb, group, NY, group * (NY * 2 * LOCAL), 2 * LOCAL, ROWS_A, ROWS_B)

    def wait_sib_a(k, slot):
        a_sib(slot, along_y(k), 1 - core).wait_recv()

    def wait_sib_b(k, slot):
        b_sib(slot, along_x(k), 1 - core).wait_recv()

    own_a.wait()
    for c in a1:
        c.wait_recv()
    go(a_right(0, 0, NX, y))
    go(a_left(0, 0, NX, y))
    go(a_sib(0, y, core))

    acc[...] = jnp.zeros_like(acc)
    sq[...] = jnp.zeros_like(sq)
    for p in params:
        p.wait()
    first_token = block * ROWS
    start, first_in, last_in, last_before = jnp.int32(0), jnp.int32(ROWS), jnp.int32(-1), jnp.int32(-1)
    starts = []
    for i in range(docs.shape[0]):
        here = start - first_token
        starts.append(here)
        inside = jnp.logical_and(here >= 0, here < ROWS)
        first_in = jnp.where(inside, jnp.minimum(first_in, here), first_in)
        last_in = jnp.where(inside, jnp.maximum(last_in, here), last_in)
        last_before = jnp.where(here < 0, jnp.maximum(last_before, start), last_before)
        start = start + docs[i]
    rate = pole[...]
    lam = jnp.exp(-rate)
    r2 = rate * rate
    series = 2.0 * jnp.exp(-rate) * rate * (
        1.0 + r2 * (1.0 / 6.0) * (1.0 + r2 * (1.0 / 20.0) * (1.0 + r2 * (1.0 / 42.0) * (1.0 + r2 * (1.0 / 72.0))))
    )
    mix = resid[...] * jnp.sqrt(jnp.where(rate < 0.5, series, 1.0 - jnp.exp(-2.0 * rate)))

    def end_weight(t, _):
        on = jnp.where(t >= last_in, 1.0, 0.0)
        sw[t] = jnp.exp(rate * (t - (ROWS - 1)).astype(F32)) * on
        return 0

    lax.fori_loop(0, ROWS, end_weight, 0, unroll=4)

    own_b.wait()
    for k in range(1, NY):
        b1[k].wait_recv()
    go(b_right(0, 0, NY, x))
    go(b_left(0, 0, NY, x))
    go(b_sib(0, x, core))

    a_right(0, 0, NX, along_y(-1)).wait_recv()
    go(a_right(1, 0, NX, along_y(-1)))
    go(a_sib(1, along_y(-1), core))
    a_left(0, 0, NX, along_y(1)).wait_recv()
    go(a_left(1, 0, NX, along_y(1)))
    go(a_sib(2, along_y(1), core))

    def from_before(t, _):
        on = jnp.where(t < first_in, 1.0, 0.0)
        t2[t] = mix * jnp.exp(rate * (-1 - t).astype(F32)) * on
        return 0

    lax.fori_loop(0, ROWS, from_before, 0, unroll=4)

    for p in parts:
        p.wait()
    wait_sib_a(0, 0)
    dots_a(0)

    a_right(1, 0, NX, along_y(-2)).wait_recv()
    go(a_right(2, 0, NX, along_y(-2)))
    go(a_sib(3, along_y(-2), core))
    a_left(1, 0, NX, along_y(2)).wait_recv()
    go(a_left(2, 0, NX, along_y(2)))
    go(a_sib(4, along_y(2), core))

    def decay(t, _):
        is_start = functools.reduce(jnp.logical_or, [t == s for s in starts])
        lk[t] = lam * jnp.where(is_start, 0.0, 1.0)
        return 0

    lax.fori_loop(0, ROWS, decay, 0, unroll=4)

    b_right(0, 0, NY, along_x(-1)).wait_recv()
    go(b_right(1, 0, NY // 2, along_x(-1)))
    go(b_sib(1, along_x(-1), core))
    b_left(0, 0, NY, along_x(1)).wait_recv()
    go(b_left(1, NY // 2, NY, along_x(1)))
    go(b_sib(2, along_x(1), core))

    wait_sib_a(-1, 1)
    dots_a(-1)
    wait_sib_a(1, 2)
    dots_a(1)
    wait_sib_b(0, 0)
    dots_b(0)

    a_right(2, 0, NX, along_y(-3)).wait_recv()
    go(a_right(3, 0, NX // 2, along_y(-3)))
    go(a_sib(5, along_y(-3), core))
    a_left(2, 0, NX, along_y(3)).wait_recv()
    go(a_left(3, NX // 2, NX, along_y(3)))
    go(a_sib(6, along_y(3), core))

    for d in range(1, REACH + 1):
        on = jnp.where(last_before < first_token - (d - 1) * ROWS, 1.0, 0.0)
        gains[d - 1] = jnp.exp(rate * (-(d - 1.0) * ROWS)) * on

    wait_sib_a(-2, 3)
    dots_a(-2)
    wait_sib_a(2, 4)
    dots_a(2)

    a_right(3, 0, NX // 2, along_y(4)).wait_recv()
    a_left(3, NX // 2, NX, along_y(4)).wait_recv()
    go(a_sib(7, along_y(4), core))
    wait_sib_b(-1, 1)
    dots_b(-1)
    b_right(1, 0, NY // 2, along_x(2)).wait_recv()
    b_left(1, NY // 2, NY, along_x(2)).wait_recv()
    go(b_sib(3, along_x(2), core))
    wait_sib_b(1, 2)
    dots_b(1)
    wait_sib_a(-3, 5)
    dots_a(-3)
    wait_sib_a(3, 6)
    dots_a(3)
    wait_sib_a(4, 7)
    dots_a(4)
    wait_sib_b(2, 3)
    dots_b(2)

    rowscale = lax.rsqrt(jnp.sum(sq[...], axis=1, keepdims=True) / width + 1e-06)
    drv[...] = (acc[:, LOCAL:2 * LOCAL] * rowscale) * (acc[:, 2 * LOCAL:] * rowscale)

    def end_state(i, carry):
        even, odd = carry
        rows = drv[pl.ds(pl.multiple_of(i * 8, 8), 8), :]
        for r in range(0, 8, 2):
            even = even + sw[i * 8 + r] * rows[r:r + 1, :]
            odd = odd + sw[i * 8 + r + 1] * rows[r + 1:r + 2, :]
        return even, odd

    nought = jnp.zeros((MODES, LOCAL), F32)
    even, odd = lax.fori_loop(0, ROWS // 8, end_state, (nought, nought), unroll=2)
    mine[...] = even + odd
    zs = [
        remote(mine, got.at[d - 1], z_send.at[d - 1], z_recv.at[d - 1], {"ctx": along_z(d)})
        for d in range(1, REACH + 1)
    ]
    for c in zs:
        c.start()

    def scan(i, state):
        rows = drv[pl.ds(pl.multiple_of(i * 8, 8), 8), :]
        for r in range(8):
            state = lk[i * 8 + r] * state + rows[r:r + 1, :]
            terms = mix * state
            y8[pl.ds(pl.multiple_of((i * 8 + r) * 8, 8), 8), :] = terms[:8] + terms[8:]
        return state

    lax.fori_loop(0, ROWS // 8, scan, nought)
    drv[...] = skip[...] * drv[...] + functools.reduce(
        jnp.add, [y8[pl.ds(s, ROWS, stride=8), :] for s in range(8)]
    )
    acc[:, :LOCAL] = acc[:, :LOCAL] * rowscale

    before = nought
    for d in range(1, REACH + 1):
        zs[d - 1].wait_recv()
        before = before + gains[d - 1] * got[d - 1]

    def carried(t, _):
        terms = t2[t] * before
        y8[pl.ds(pl.multiple_of(t * 8, 8), 8), :] = terms[:8] + terms[8:]
        return 0

    lax.fori_loop(0, ROWS, carried, 0, unroll=8)
    total = drv[...] + functools.reduce(
        jnp.add, [y8[pl.ds(s, ROWS, stride=8), :] for s in range(8)]
    )
    out[...] = (acc[:, :LOCAL] * total).astype(out.dtype)

    for c in (*a1, *b1.values(), *sent, *zs):
        c.wait_send()


def per_device(n_ctx, stream, in_weight, pole_rate, residue, skip_gain, doc_lengths):
    width = in_weight.shape[0]
    hbm = pl.BlockSpec(memory_space=pltpu.MemorySpace.HBM)
    dma = pltpu.SemaphoreType.DMA
    vmem = pltpu.VMEM
    bf16 = jnp.bfloat16
    return pl.pallas_call(
        functools.partial(kernel, n_ctx, width),
        out_shape=jax.ShapeDtypeStruct((ROWS, LOCAL), bf16),
        in_specs=[hbm] * 6,
        out_specs=pl.BlockSpec(memory_space=pltpu.VMEM),
        scratch_shapes=[
            vmem((NY, 2, NX, ROWS_A, LOCAL), bf16),
            vmem((NX, 2, NY, ROWS_B, LOCAL), bf16),
            vmem((width, 3 * LOCAL), bf16),
            vmem((ROWS, 3 * LOCAL), F32),
            vmem((ROWS, LOCAL), F32),
            vmem((ROWS, LOCAL), F32),
            vmem((ROWS * 8, LOCAL), F32),
            vmem((ROWS, MODES, LOCAL), F32),
            vmem((ROWS, MODES, LOCAL), F32),
            vmem((ROWS, MODES, LOCAL), F32),
            vmem((MODES, LOCAL), F32),
            vmem((MODES, LOCAL), F32),
            vmem((1, LOCAL), F32),
            vmem((MODES, LOCAL), F32),
            vmem((REACH, MODES, LOCAL), F32),
            vmem((REACH, MODES, LOCAL), F32),
            pltpu.SMEM((doc_lengths.shape[0],), jnp.int32),
            dma((3,)), dma((4,)), dma((2,)),
            dma((NX - 1,)), dma((NX - 1,)), dma((NY - 1,)), dma((NY - 1,)),
            dma((4,)), dma((4,)), dma((4,)), dma((4,)),
            dma((2,)), dma((2,)), dma((2,)), dma((2,)),
            dma((NY,)), dma((NY,)), dma((NX,)), dma((NX,)),
            dma((REACH,)), dma((REACH,)),
        ],
        compiler_params=pltpu.CompilerParams(
            collective_id=0, has_side_effects=True, vmem_limit_bytes=40 << 20
        ),
        name="hyena",
    )(
        stream, jnp.transpose(in_weight, (1, 0, 2)), pole_rate.T, residue.T,
        skip_gain.reshape(1, LOCAL), doc_lengths,
    )


def solution(mesh):
    placed = (P("ctx", "ch"), P(None, None, "ch"), P("ch", None), P("ch", None), P("ch"), P())
    return jax.shard_map(
        functools.partial(per_device, mesh.shape["ctx"]),
        mesh=mesh, in_specs=placed, out_specs=P("ctx", "ch"), check_vma=False,
    )
```

```python
import functools

import jax
import jax.numpy as jnp
from jax import lax
from jax.experimental import pallas as pl
from jax.experimental.pallas import tpu as pltpu
from jax.sharding import PartitionSpec as P

MESH = pl.DeviceIdType.MESH
NX, NY = 4, 8
ROWS = 128
LOCAL = 128
MODES = 16
ROWS_A = 64
ROWS_B = ROWS - ROWS_A
REACH = 6
F32 = jnp.float32


def kernel(
    n_ctx, width,
    stream, w3, pole_h, resid_h, skip_h, docs_h, out,
    ga, gb, w, acc, sq, drv, y8, sw, lk, t2, pole, resid, skip, mine, got, gains, docs,
    w_sem, prm_sem, own_sem,
    a1_send, a1_recv, b1_send, b1_recv,
    ar_send, ar_recv, al_send, al_recv,
    br_send, br_recv, bl_send, bl_recv,
    as_send, as_recv, bs_send, bs_recv,
    z_send, z_recv, z_ready,
):
    block = lax.axis_index("ctx")
    ch = lax.axis_index("ch")
    core = lax.rem(ch, 2)
    y = lax.rem(ch // 2, NY)
    x = ch // (2 * NY)

    def at(px, py, pc):
        return {"ch": (px * NY + py) * 2 + pc}

    def along_x(k):
        return lax.rem(x + (k + NX), NX)

    def along_y(k):
        return lax.rem(y + (k + NY), NY)

    def remote(src, dst, send, recv, device):
        return pltpu.make_async_remote_copy(
            src_ref=src, dst_ref=dst, send_sem=send, recv_sem=recv,
            device_id=device, device_id_type=MESH,
        )

    parts = [
        pltpu.make_async_copy(w3.at[j], w.at[:, pl.ds(j * LOCAL, LOCAL)], w_sem.at[j])
        for j in range(3)
    ]
    params = [
        pltpu.make_async_copy(src, dst, prm_sem.at[i])
        for i, (src, dst) in enumerate(
            ((pole_h, pole), (resid_h, resid), (skip_h, skip), (docs_h, docs))
        )
    ]
    own_a = pltpu.make_async_copy(stream.at[pl.ds(0, ROWS_A)], ga.at[y, core, x], own_sem.at[0])
    own_b = pltpu.make_async_copy(stream.at[pl.ds(ROWS_A, ROWS_B)], gb.at[x, core, y], own_sem.at[1])
    own_a.start()
    own_b.start()
    for p in params:
        p.start()

    sibling = at(x, y, 1 - core)
    friends = [sibling]
    friends += [at(along_x(k), y, core) for k in range(1, NX)]
    friends += [at(x, along_y(k), core) for k in range(1, NY)]
    barrier = pltpu.get_barrier_semaphore()
    for friend in friends:
        pl.semaphore_signal(barrier, inc=1, device_id=friend, device_id_type=MESH)

    def if_later(d, action):
        pl.when(block + d < n_ctx)(action)

    def if_earlier(d, action):
        pl.when(block >= d)(action)

    for d in range(1, REACH + 1):
        if_later(d, lambda d=d: pl.semaphore_signal(
            barrier, inc=1, device_id={"ctx": block + d}, device_id_type=MESH))
    for p in parts:
        p.start()
    got[...] = jnp.zeros_like(got)
    pl.semaphore_wait(barrier, len(friends) + jnp.minimum(block, REACH))

    a1 = [
        remote(stream.at[pl.ds(0, ROWS_A)], ga.at[y, core, x],
               a1_send.at[k - 1], a1_recv.at[k - 1], at(along_x(k), y, core))
        for k in range(1, NX)
    ]
    b1 = {
        k: remote(stream.at[pl.ds(ROWS_A, ROWS_B)], gb.at[x, core, y],
                  b1_send.at[k - 1], b1_recv.at[k - 1], at(x, along_y(k), core))
        for k in range(1, NY)
    }
    for c in a1:
        c.start()
    for k in (1, 7, 2, 6, 3, 5, 4):
        b1[k].start()

    for d in range(1, REACH + 1):
        if_earlier(d, lambda d=d: pl.semaphore_signal(
            z_ready.at[d - 1], inc=1, device_id={"ctx": block - d}, device_id_type=MESH))

    sent = []

    def go(copy):
        copy.start()
        sent.append(copy)

    def a_right(step, lo, hi, group):
        ref = ga.at[group, core, pl.ds(lo, hi - lo)]
        return remote(ref, ref, ar_send.at[step], ar_recv.at[step], at(x, along_y(1), core))

    def a_left(step, lo, hi, group):
        ref = ga.at[group, core, pl.ds(lo, hi - lo)]
        return remote(ref, ref, al_send.at[step], al_recv.at[step], at(x, along_y(-1), core))

    def b_right(step, lo, hi, group):
        ref = gb.at[group, core, pl.ds(lo, hi - lo)]
        return remote(ref, ref, br_send.at[step], br_recv.at[step], at(along_x(1), y, core))

    def b_left(step, lo, hi, group):
        ref = gb.at[group, core, pl.ds(lo, hi - lo)]
        return remote(ref, ref, bl_send.at[step], bl_recv.at[step], at(along_x(-1), y, core))

    def a_sib(k, group, c):
        ref = ga.at[group, c]
        return remote(ref, ref, as_send.at[k], as_recv.at[k], sibling)

    def b_sib(k, group, c):
        ref = gb.at[group, c]
        return remote(ref, ref, bs_send.at[k], bs_recv.at[k], sibling)

    def add_group(buf, group, count, base, stride, lo, rows):
        def body(i, carry):
            total, squares = carry
            lhs = jnp.concatenate([buf[group, 0, i], buf[group, 1, i]], axis=1)
            first = pl.multiple_of(base + i * stride, 2 * LOCAL)
            total = total + jnp.dot(lhs, w[pl.ds(first, 2 * LOCAL), :], preferred_element_type=F32)
            f = lhs.astype(F32)
            f = f * f
            return total, squares + (f[:, :LOCAL] + f[:, LOCAL:])

        where = pl.ds(lo, rows)
        total, squares = lax.fori_loop(0, count, body, (acc[where, :], sq[where, :]))
        acc[where, :] = total
        sq[where, :] = squares

    def dots_a(k):
        group = along_y(k)
        add_group(ga, group, NX, group * (2 * LOCAL), NY * 2 * LOCAL, 0, ROWS_A)

    def dots_b(k):
        group = along_x(k)
        add_group(gb, group, NY, group * (NY * 2 * LOCAL), 2 * LOCAL, ROWS_A, ROWS_B)

    def wait_sib_a(k, slot):
        a_sib(slot, along_y(k), 1 - core).wait_recv()

    def wait_sib_b(k, slot):
        b_sib(slot, along_x(k), 1 - core).wait_recv()

    own_a.wait()
    for c in a1:
        c.wait_recv()
    go(a_right(0, 0, NX, y))
    go(a_left(0, 0, NX, y))
    go(a_sib(0, y, core))

    acc[...] = jnp.zeros_like(acc)
    sq[...] = jnp.zeros_like(sq)
    for p in params:
        p.wait()
    first_token = block * ROWS
    start, first_in, last_in, last_before = jnp.int32(0), jnp.int32(ROWS), jnp.int32(-1), jnp.int32(-1)
    starts = []
    for i in range(docs.shape[0]):
        here = start - first_token
        starts.append(here)
        inside = jnp.logical_and(here >= 0, here < ROWS)
        first_in = jnp.where(inside, jnp.minimum(first_in, here), first_in)
        last_in = jnp.where(inside, jnp.maximum(last_in, here), last_in)
        last_before = jnp.where(here < 0, jnp.maximum(last_before, start), last_before)
        start = start + docs[i]
    rate = pole[...]
    lam = jnp.exp(-rate)
    r2 = rate * rate
    series = 2.0 * jnp.exp(-rate) * rate * (
        1.0 + r2 * (1.0 / 6.0) * (1.0 + r2 * (1.0 / 20.0) * (1.0 + r2 * (1.0 / 42.0) * (1.0 + r2 * (1.0 / 72.0))))
    )
    mix = resid[...] * jnp.sqrt(jnp.where(rate < 0.5, series, 1.0 - jnp.exp(-2.0 * rate)))

    def end_weight(t, _):
        on = jnp.where(t >= last_in, 1.0, 0.0)
        sw[t] = jnp.exp(rate * (t - (ROWS - 1)).astype(F32)) * on
        return 0

    lax.fori_loop(0, ROWS, end_weight, 0, unroll=4)

    own_b.wait()
    for k in range(1, NY):
        b1[k].wait_recv()
    go(b_right(0, 0, NY, x))
    go(b_left(0, 0, NY, x))
    go(b_sib(0, x, core))

    a_right(0, 0, NX, along_y(-1)).wait_recv()
    go(a_right(1, 0, NX, along_y(-1)))
    go(a_sib(1, along_y(-1), core))
    a_left(0, 0, NX, along_y(1)).wait_recv()
    go(a_left(1, 0, NX, along_y(1)))
    go(a_sib(2, along_y(1), core))

    def from_before(t, _):
        on = jnp.where(t < first_in, 1.0, 0.0)
        t2[t] = mix * jnp.exp(rate * (-1 - t).astype(F32)) * on
        return 0

    lax.fori_loop(0, ROWS, from_before, 0, unroll=4)

    for p in parts:
        p.wait()
    wait_sib_a(0, 0)
    dots_a(0)

    a_right(1, 0, NX, along_y(-2)).wait_recv()
    go(a_right(2, 0, NX, along_y(-2)))
    go(a_sib(3, along_y(-2), core))
    a_left(1, 0, NX, along_y(2)).wait_recv()
    go(a_left(2, 0, NX, along_y(2)))
    go(a_sib(4, along_y(2), core))

    def decay(t, _):
        is_start = functools.reduce(jnp.logical_or, [t == s for s in starts])
        lk[t] = lam * jnp.where(is_start, 0.0, 1.0)
        return 0

    lax.fori_loop(0, ROWS, decay, 0, unroll=4)

    b_right(0, 0, NY, along_x(-1)).wait_recv()
    go(b_right(1, 0, NY // 2, along_x(-1)))
    go(b_sib(1, along_x(-1), core))
    b_left(0, 0, NY, along_x(1)).wait_recv()
    go(b_left(1, NY // 2, NY, along_x(1)))
    go(b_sib(2, along_x(1), core))

    wait_sib_a(-1, 1)
    dots_a(-1)
    wait_sib_a(1, 2)
    dots_a(1)
    wait_sib_b(0, 0)
    dots_b(0)

    a_right(2, 0, NX, along_y(-3)).wait_recv()
    go(a_right(3, 0, NX // 2, along_y(-3)))
    go(a_sib(5, along_y(-3), core))
    a_left(2, 0, NX, along_y(3)).wait_recv()
    go(a_left(3, NX // 2, NX, along_y(3)))
    go(a_sib(6, along_y(3), core))

    for d in range(1, REACH + 1):
        on = jnp.where(last_before < first_token - (d - 1) * ROWS, 1.0, 0.0)
        gains[d - 1] = jnp.exp(rate * (-(d - 1.0) * ROWS)) * on

    wait_sib_a(-2, 3)
    dots_a(-2)
    wait_sib_a(2, 4)
    dots_a(2)

    a_right(3, 0, NX // 2, along_y(4)).wait_recv()
    a_left(3, NX // 2, NX, along_y(4)).wait_recv()
    go(a_sib(7, along_y(4), core))
    wait_sib_b(-1, 1)
    dots_b(-1)
    b_right(1, 0, NY // 2, along_x(2)).wait_recv()
    b_left(1, NY // 2, NY, along_x(2)).wait_recv()
    go(b_sib(3, along_x(2), core))
    wait_sib_b(1, 2)
    dots_b(1)
    wait_sib_a(-3, 5)
    dots_a(-3)
    wait_sib_a(3, 6)
    dots_a(3)
    wait_sib_a(4, 7)
    dots_a(4)
    wait_sib_b(2, 3)
    dots_b(2)

    rowscale = lax.rsqrt(jnp.sum(sq[...], axis=1, keepdims=True) / width + 1e-06)
    drv[...] = (acc[:, LOCAL:2 * LOCAL] * rowscale) * (acc[:, 2 * LOCAL:] * rowscale)

    def end_state(i, carry):
        even, odd = carry
        rows = drv[pl.ds(pl.multiple_of(i * 8, 8), 8), :]
        for r in range(0, 8, 2):
            even = even + sw[i * 8 + r] * rows[r:r + 1, :]
            odd = odd + sw[i * 8 + r + 1] * rows[r + 1:r + 2, :]
        return even, odd

    nought = jnp.zeros((MODES, LOCAL), F32)
    even, odd = lax.fori_loop(0, ROWS // 8, end_state, (nought, nought), unroll=2)
    mine[...] = even + odd
    zs = [
        remote(mine, got.at[d - 1], z_send.at[d - 1], z_recv.at[d - 1], {"ctx": block + d})
        for d in range(1, REACH + 1)
    ]
    for d in range(1, REACH + 1):
        def to_later(d=d):
            pl.semaphore_wait(z_ready.at[d - 1], 1)
            zs[d - 1].start()
        if_later(d, to_later)

    def scan(i, state):
        rows = drv[pl.ds(pl.multiple_of(i * 8, 8), 8), :]
        for r in range(8):
            state = lk[i * 8 + r] * state + rows[r:r + 1, :]
            terms = mix * state
            y8[pl.ds(pl.multiple_of((i * 8 + r) * 8, 8), 8), :] = terms[:8] + terms[8:]
        return state

    lax.fori_loop(0, ROWS // 8, scan, nought)
    drv[...] = skip[...] * drv[...] + functools.reduce(
        jnp.add, [y8[pl.ds(s, ROWS, stride=8), :] for s in range(8)]
    )
    acc[:, :LOCAL] = acc[:, :LOCAL] * rowscale

    before = nought
    for d in range(1, REACH + 1):
        if_earlier(d, zs[d - 1].wait_recv)
        before = before + gains[d - 1] * got[d - 1]

    def carried(t, _):
        terms = t2[t] * before
        y8[pl.ds(pl.multiple_of(t * 8, 8), 8), :] = terms[:8] + terms[8:]
        return 0

    lax.fori_loop(0, ROWS, carried, 0, unroll=8)
    total = drv[...] + functools.reduce(
        jnp.add, [y8[pl.ds(s, ROWS, stride=8), :] for s in range(8)]
    )
    out[...] = (acc[:, :LOCAL] * total).astype(out.dtype)

    for c in (*a1, *b1.values(), *sent):
        c.wait_send()
    for d in range(1, REACH + 1):
        if_later(d, zs[d - 1].wait_send)


def per_device(n_ctx, stream, in_weight, pole_rate, residue, skip_gain, doc_lengths):
    width = in_weight.shape[0]
    hbm = pl.BlockSpec(memory_space=pltpu.MemorySpace.HBM)
    dma = pltpu.SemaphoreType.DMA
    vmem = pltpu.VMEM
    bf16 = jnp.bfloat16
    return pl.pallas_call(
        functools.partial(kernel, n_ctx, width),
        out_shape=jax.ShapeDtypeStruct((ROWS, LOCAL), bf16),
        in_specs=[hbm] * 6,
        out_specs=pl.BlockSpec(memory_space=pltpu.VMEM),
        scratch_shapes=[
            vmem((NY, 2, NX, ROWS_A, LOCAL), bf16),
            vmem((NX, 2, NY, ROWS_B, LOCAL), bf16),
            vmem((width, 3 * LOCAL), bf16),
            vmem((ROWS, 3 * LOCAL), F32),
            vmem((ROWS, LOCAL), F32),
            vmem((ROWS, LOCAL), F32),
            vmem((ROWS * 8, LOCAL), F32),
            vmem((ROWS, MODES, LOCAL), F32),
            vmem((ROWS, MODES, LOCAL), F32),
            vmem((ROWS, MODES, LOCAL), F32),
            vmem((MODES, LOCAL), F32),
            vmem((MODES, LOCAL), F32),
            vmem((1, LOCAL), F32),
            vmem((MODES, LOCAL), F32),
            vmem((REACH, MODES, LOCAL), F32),
            vmem((REACH, MODES, LOCAL), F32),
            pltpu.SMEM((doc_lengths.shape[0],), jnp.int32),
            dma((3,)), dma((4,)), dma((2,)),
            dma((NX - 1,)), dma((NX - 1,)), dma((NY - 1,)), dma((NY - 1,)),
            dma((4,)), dma((4,)), dma((4,)), dma((4,)),
            dma((2,)), dma((2,)), dma((2,)), dma((2,)),
            dma((NY,)), dma((NY,)), dma((NX,)), dma((NX,)),
            dma((REACH,)), dma((REACH,)), pltpu.SemaphoreType.REGULAR((REACH,)),
        ],
        compiler_params=pltpu.CompilerParams(
            collective_id=0, has_side_effects=True, vmem_limit_bytes=60 << 20
        ),
        name="hyena",
    )(
        stream, jnp.transpose(in_weight, (1, 0, 2)), pole_rate.T, residue.T,
        skip_gain.reshape(1, LOCAL), doc_lengths,
    )


def solution(mesh):
    placed = (P("ctx", "ch"), P(None, None, "ch"), P("ch", None), P("ch", None), P("ch"), P())
    return jax.shard_map(
        functools.partial(per_device, mesh.shape["ctx"]),
        mesh=mesh, in_specs=placed, out_specs=P("ctx", "ch"), check_vma=False,
    )
```

```python
import functools

import jax
import jax.numpy as jnp
from jax import lax
from jax.experimental import pallas as pl
from jax.experimental.pallas import tpu as pltpu
from jax.sharding import PartitionSpec as P

MESH = pl.DeviceIdType.MESH
NX, NY = 4, 8
ROWS = 128
LOCAL = 128
MODES = 16
OFFSETS = (0, 1, -1, 2, -2, 3, -3, 4)
GROUPS = ((0, 1), (1, 3), (3, 5), (5, 7), (7, 8))
COLUMNS = (0, 1, -1, 2)
REACH = 6
F32 = jnp.float32


def kernel(
    n_ctx, width,
    stream, w3, pole_h, resid_h, skip_h, docs_h, out,
    g, w, acc, sq, drv, y8, sw, lk, t2, pole, resid, skip, mine, got, gains, docs,
    w_sem, prm_sem, own_sem,
    y_send, y_recv, xr_send, xr_recv, xl_send, xl_recv,
    x2r_send, x2r_recv, x2l_send, x2l_recv,
    s0_send, s0_recv, s1_send, s1_recv, s2_send, s2_recv,
    z_send, z_recv, z_ready,
):
    block = lax.axis_index("ctx")
    ch = lax.axis_index("ch")
    core = lax.rem(ch, 2)
    y = lax.rem(ch // 2, NY)
    x = ch // (2 * NY)

    def at(px, py, pc):
        return {"ch": (px * NY + py) * 2 + pc}

    def along_x(k):
        return lax.rem(x + (k + NX), NX)

    def along_y(k):
        return lax.rem(y + (k + NY), NY)

    def remote(src, dst, send, recv, device):
        return pltpu.make_async_remote_copy(
            src_ref=src, dst_ref=dst, send_sem=send, recv_sem=recv,
            device_id=device, device_id_type=MESH,
        )

    parts = [
        pltpu.make_async_copy(w3.at[j], w.at[:, pl.ds(j * LOCAL, LOCAL)], w_sem.at[j])
        for j in range(3)
    ]
    params = [
        pltpu.make_async_copy(src, dst, prm_sem.at[i])
        for i, (src, dst) in enumerate(
            ((pole_h, pole), (resid_h, resid), (skip_h, skip), (docs_h, docs))
        )
    ]
    own = pltpu.make_async_copy(stream, g.at[core, 0, 0], own_sem)
    own.start()
    for p in params:
        p.start()

    sibling = at(x, y, 1 - core)
    friends = [sibling]
    friends += [at(along_x(k), y, core) for k in (1, -1)]
    friends += [at(x, along_y(k), core) for k in range(1, NY)]
    barrier = pltpu.get_barrier_semaphore()
    for friend in friends:
        pl.semaphore_signal(barrier, inc=1, device_id=friend, device_id_type=MESH)

    def if_later(d, action):
        pl.when(block + d < n_ctx)(action)

    def if_earlier(d, action):
        pl.when(block >= d)(action)

    for d in range(1, REACH + 1):
        if_later(d, lambda d=d: pl.semaphore_signal(
            barrier, inc=1, device_id={"ctx": block + d}, device_id_type=MESH))
    for p in parts:
        p.start()
    got[...] = jnp.zeros_like(got)
    pl.semaphore_wait(barrier, len(friends) + jnp.minimum(block, REACH))

    sent = []

    def go(copy):
        copy.start()
        sent.append(copy)

    def same(ref, send, recv, device):
        return remote(ref, ref, send, recv, device)

    def y_copy(k):
        slot = OFFSETS.index(-k if k < 4 else 4)
        return remote(stream, g.at[core, 0, slot], y_send.at[slot - 1], y_recv.at[slot - 1],
                      at(x, along_y(k), core))

    def x_right(i):
        lo, hi = GROUPS[i]
        src = stream if i == 0 else g.at[core, 0, pl.ds(lo, hi - lo)]
        dst = g.at[core, 2, 0] if i == 0 else g.at[core, 2, pl.ds(lo, hi - lo)]
        return remote(src, dst, xr_send.at[i], xr_recv.at[i], at(along_x(1), y, core))

    def x_left(i):
        lo, hi = GROUPS[i]
        src = stream if i == 0 else g.at[core, 0, pl.ds(lo, hi - lo)]
        dst = g.at[core, 1, 0] if i == 0 else g.at[core, 1, pl.ds(lo, hi - lo)]
        return remote(src, dst, xl_send.at[i], xl_recv.at[i], at(along_x(-1), y, core))

    def half(column, i, side):
        lo, hi = GROUPS[i]
        if hi - lo == 2:
            return g.at[core, column, lo + side]
        return g.at[core, column, lo, pl.ds(side * (ROWS // 2), ROWS // 2)]

    def x2_right(i):
        return remote(half(2, i, 0), half(3, i, 0), x2r_send.at[i], x2r_recv.at[i], at(along_x(1), y, core))

    def x2_left(i):
        return remote(half(1, i, 1), half(3, i, 1), x2l_send.at[i], x2l_recv.at[i], at(along_x(-1), y, core))

    def sib(column, i, c):
        lo, hi = GROUPS[i]
        slots = pl.ds(lo, hi - lo)
        if column == 0:
            return same(g.at[c, 0, slots], s0_send.at[i], s0_recv.at[i], sibling)
        if column == 1:
            return same(g.at[c, pl.ds(1, 2), slots], s1_send.at[i], s1_recv.at[i], sibling)
        return same(g.at[c, 3, slots], s2_send.at[i], s2_recv.at[i], sibling)

    go(x_right(0))
    go(x_left(0))
    for k in (1, -1, 2, -2, 3, -3, 4):
        go(y_copy(k))
    for d in range(1, REACH + 1):
        if_earlier(d, lambda d=d: pl.semaphore_signal(
            z_ready.at[d - 1], inc=1, device_id={"ctx": block - d}, device_id_type=MESH))

    own.wait()
    go(sib(0, 0, core))

    def dots(column, i):
        columns = (1, 2) if column == 1 else (column,)
        for c in columns:
            for slot in range(*GROUPS[i]):
                chip = along_x(COLUMNS[c]) * NY + along_y(OFFSETS[slot])
                lhs = jnp.concatenate([g[0, c, slot], g[1, c, slot]], axis=1)
                rows = pl.ds(pl.multiple_of(chip * (2 * LOCAL), 2 * LOCAL), 2 * LOCAL)
                acc[...] += jnp.dot(lhs, w[rows, :], preferred_element_type=F32)
                f = lhs.astype(F32)
                f = f * f
                sq[...] += f[:, :LOCAL] + f[:, LOCAL:]

    def col0(i):
        for slot in range(*GROUPS[i]):
            k = OFFSETS[slot]
            y_copy(4 if k == 4 else -k).wait_recv()
        go(x_right(i))
        go(x_left(i))
        go(sib(0, i, core))

    def col1(i):
        x_right(i).wait_recv()
        go(x2_right(i))
        x_left(i).wait_recv()
        go(x2_left(i))
        go(sib(1, i, core))

    def col2(i):
        x2_right(i).wait_recv()
        x2_left(i).wait_recv()
        go(sib(3, i, core))

    def use(column, i):
        sib(column, i, 1 - core).wait_recv()
        dots(column, i)

    acc[...] = jnp.zeros_like(acc)
    sq[...] = jnp.zeros_like(sq)
    for p in params:
        p.wait()
    first_token = block * ROWS
    start, first_in, last_in, last_before = jnp.int32(0), jnp.int32(ROWS), jnp.int32(-1), jnp.int32(-1)
    starts = []
    for i in range(docs.shape[0]):
        here = start - first_token
        starts.append(here)
        inside = jnp.logical_and(here >= 0, here < ROWS)
        first_in = jnp.where(inside, jnp.minimum(first_in, here), first_in)
        last_in = jnp.where(inside, jnp.maximum(last_in, here), last_in)
        last_before = jnp.where(here < 0, jnp.maximum(last_before, start), last_before)
        start = start + docs[i]
    rate = pole[...]
    lam = jnp.exp(-rate)
    r2 = rate * rate
    series = 2.0 * jnp.exp(-rate) * rate * (
        1.0 + r2 * (1.0 / 6.0) * (1.0 + r2 * (1.0 / 20.0) * (1.0 + r2 * (1.0 / 42.0) * (1.0 + r2 * (1.0 / 72.0))))
    )
    mix = resid[...] * jnp.sqrt(jnp.where(rate < 0.5, series, 1.0 - jnp.exp(-2.0 * rate)))

    def end_weight(t, _):
        on = jnp.where(t >= last_in, 1.0, 0.0)
        sw[t] = jnp.exp(rate * (t - (ROWS - 1)).astype(F32)) * on
        return 0

    def from_before(t, _):
        on = jnp.where(t < first_in, 1.0, 0.0)
        t2[t] = mix * jnp.exp(rate * (-1 - t).astype(F32)) * on
        return 0

    def decay(t, _):
        is_start = functools.reduce(jnp.logical_or, [t == s for s in starts])
        lk[t] = lam * jnp.where(is_start, 0.0, 1.0)
        return 0

    lax.fori_loop(0, ROWS, end_weight, 0, unroll=8)
    col0(1)
    col1(0)
    col0(2)
    lax.fori_loop(0, ROWS, from_before, 0, unroll=8)
    for p in parts:
        p.wait()
    use(0, 0)
    col1(1)
    col0(3)
    col2(0)
    use(0, 1)
    col0(4)
    col1(2)
    col2(1)
    lax.fori_loop(0, ROWS, decay, 0, unroll=8)
    for d in range(1, REACH + 1):
        on = jnp.where(last_before < first_token - (d - 1) * ROWS, 1.0, 0.0)
        gains[d - 1] = jnp.exp(rate * (-(d - 1.0) * ROWS)) * on
    use(1, 0)
    use(0, 2)
    use(3, 0)
    col1(3)
    col2(2)
    use(1, 1)
    use(0, 3)
    col1(4)
    col2(3)
    use(0, 4)
    use(3, 1)
    use(1, 2)
    use(3, 2)
    col2(4)
    use(1, 3)
    use(1, 4)
    use(3, 3)
    use(3, 4)

    rowscale = lax.rsqrt(jnp.sum(sq[...], axis=1, keepdims=True) / width + 1e-06)
    drv[...] = (acc[:, LOCAL:2 * LOCAL] * rowscale) * (acc[:, 2 * LOCAL:] * rowscale)

    def end_state(i, carry):
        even, odd = carry
        rows = drv[pl.ds(pl.multiple_of(i * 8, 8), 8), :]
        for r in range(0, 8, 2):
            even = even + sw[i * 8 + r] * rows[r:r + 1, :]
            odd = odd + sw[i * 8 + r + 1] * rows[r + 1:r + 2, :]
        return even, odd

    nought = jnp.zeros((MODES, LOCAL), F32)
    even, odd = lax.fori_loop(0, ROWS // 8, end_state, (nought, nought), unroll=2)
    mine[...] = even + odd
    zs = [
        remote(mine, got.at[d - 1], z_send.at[d - 1], z_recv.at[d - 1], {"ctx": block + d})
        for d in range(1, REACH + 1)
    ]
    for d in range(1, REACH + 1):
        def to_later(d=d):
            pl.semaphore_wait(z_ready.at[d - 1], 1)
            zs[d - 1].start()
        if_later(d, to_later)

    def scan(i, state):
        rows = drv[pl.ds(pl.multiple_of(i * 8, 8), 8), :]
        for r in range(8):
            state = lk[i * 8 + r] * state + rows[r:r + 1, :]
            terms = mix * state
            y8[pl.ds(pl.multiple_of((i * 8 + r) * 8, 8), 8), :] = terms[:8] + terms[8:]
        return state

    lax.fori_loop(0, ROWS // 8, scan, nought)
    drv[...] = skip[...] * drv[...] + functools.reduce(
        jnp.add, [y8[pl.ds(s, ROWS, stride=8), :] for s in range(8)]
    )
    acc[:, :LOCAL] = acc[:, :LOCAL] * rowscale

    before = nought
    for d in range(1, REACH + 1):
        if_earlier(d, zs[d - 1].wait_recv)
        before = before + gains[d - 1] * got[d - 1]

    def carried(t, _):
        terms = t2[t] * before
        y8[pl.ds(pl.multiple_of(t * 8, 8), 8), :] = terms[:8] + terms[8:]
        return 0

    lax.fori_loop(0, ROWS, carried, 0, unroll=8)
    total = drv[...] + functools.reduce(
        jnp.add, [y8[pl.ds(s, ROWS, stride=8), :] for s in range(8)]
    )
    out[...] = (acc[:, :LOCAL] * total).astype(out.dtype)

    for c in sent:
        c.wait_send()
    for d in range(1, REACH + 1):
        if_later(d, zs[d - 1].wait_send)


def per_device(n_ctx, stream, in_weight, pole_rate, residue, skip_gain, doc_lengths):
    width = in_weight.shape[0]
    hbm = pl.BlockSpec(memory_space=pltpu.MemorySpace.HBM)
    dma = pltpu.SemaphoreType.DMA
    vmem = pltpu.VMEM
    bf16 = jnp.bfloat16
    return pl.pallas_call(
        functools.partial(kernel, n_ctx, width),
        out_shape=jax.ShapeDtypeStruct((ROWS, LOCAL), bf16),
        in_specs=[hbm] * 6,
        out_specs=pl.BlockSpec(memory_space=pltpu.VMEM),
        scratch_shapes=[
            vmem((2, NX, NY, ROWS, LOCAL), bf16),
            vmem((width, 3 * LOCAL), bf16),
            vmem((ROWS, 3 * LOCAL), F32),
            vmem((ROWS, LOCAL), F32),
            vmem((ROWS, LOCAL), F32),
            vmem((ROWS * 8, LOCAL), F32),
            vmem((ROWS, MODES, LOCAL), F32),
            vmem((ROWS, MODES, LOCAL), F32),
            vmem((ROWS, MODES, LOCAL), F32),
            vmem((MODES, LOCAL), F32),
            vmem((MODES, LOCAL), F32),
            vmem((1, LOCAL), F32),
            vmem((MODES, LOCAL), F32),
            vmem((REACH, MODES, LOCAL), F32),
            vmem((REACH, MODES, LOCAL), F32),
            pltpu.SMEM((doc_lengths.shape[0],), jnp.int32),
            dma((3,)), dma((4,)), dma,
            dma((NY - 1,)), dma((NY - 1,)),
            *[dma((len(GROUPS),))] * 14,
            dma((REACH,)), dma((REACH,)), pltpu.SemaphoreType.REGULAR((REACH,)),
        ],
        compiler_params=pltpu.CompilerParams(
            collective_id=0, has_side_effects=True, vmem_limit_bytes=60 << 20
        ),
        name="hyena",
    )(
        stream, jnp.transpose(in_weight, (1, 0, 2)), pole_rate.T, residue.T,
        skip_gain.reshape(1, LOCAL), doc_lengths,
    )


def solution(mesh):
    placed = (P("ctx", "ch"), P(None, None, "ch"), P("ch", None), P("ch", None), P("ch"), P())
    return jax.shard_map(
        functools.partial(per_device, mesh.shape["ctx"]),
        mesh=mesh, in_specs=placed, out_specs=P("ctx", "ch"), check_vma=False,
    )
```

```python
import functools

import jax
import jax.numpy as jnp
from jax import lax
from jax.experimental import pallas as pl
from jax.experimental.pallas import tpu as pltpu
from jax.sharding import PartitionSpec as P

MESH = pl.DeviceIdType.MESH
NX, NY = 4, 8
ROWS = 128
LOCAL = 128
MODES = 16
OFFSETS = (0, 1, -1, 2, -2, 3, -3, 4)
GROUPS = ((0, 1), (1, 3), (3, 5), (5, 7), (7, 8))
BY_Y = 1
COLUMNS = (0, 1, -1, 2)
REACH = 6
F32 = jnp.float32


def kernel(
    n_ctx, width,
    stream, w3, pole_h, resid_h, skip_h, docs_h, out,
    g, w, acc, sq, drv, y8, sw, lk, t2, pole, resid, skip, mine, got, gains, docs,
    w_sem, prm_sem, own_sem,
    y_send, y_recv, x_send, x_recv, f_send, f_recv, s_send, s_recv,
    z_send, z_recv, z_ready,
):
    block = lax.axis_index("ctx")
    ch = lax.axis_index("ch")
    core = lax.rem(ch, 2)
    y = lax.rem(ch // 2, NY)
    x = ch // (2 * NY)

    def at(px, py, pc):
        return {"ch": (px * NY + py) * 2 + pc}

    def along_x(k):
        return lax.rem(x + (k + NX), NX)

    def along_y(k):
        return lax.rem(y + (k + NY), NY)

    def remote(src, dst, send, recv, device):
        return pltpu.make_async_remote_copy(
            src_ref=src, dst_ref=dst, send_sem=send, recv_sem=recv,
            device_id=device, device_id_type=MESH,
        )

    parts = [
        pltpu.make_async_copy(w3.at[j], w.at[:, pl.ds(j * LOCAL, LOCAL)], w_sem.at[j])
        for j in range(3)
    ]
    params = [
        pltpu.make_async_copy(src, dst, prm_sem.at[i])
        for i, (src, dst) in enumerate(
            ((pole_h, pole), (resid_h, resid), (skip_h, skip), (docs_h, docs))
        )
    ]
    own = pltpu.make_async_copy(stream, g.at[core, 0, 0], own_sem)
    own.start()
    for p in params:
        p.start()

    sibling = at(x, y, 1 - core)
    friends = [sibling]
    friends += [at(along_x(k), y, core) for k in (1, -1, 2)]
    friends += [at(x, along_y(k), core) for k in (1, -1, 2, -2)]
    barrier = pltpu.get_barrier_semaphore()
    for friend in friends:
        pl.semaphore_signal(barrier, inc=1, device_id=friend, device_id_type=MESH)

    def if_later(d, action):
        pl.when(block + d < n_ctx)(action)

    def if_earlier(d, action):
        pl.when(block >= d)(action)

    for d in range(1, REACH + 1):
        if_later(d, lambda d=d: pl.semaphore_signal(
            barrier, inc=1, device_id={"ctx": block + d}, device_id_type=MESH))
    own.wait()
    for p in parts:
        p.start()
    got[...] = jnp.zeros_like(got)
    pl.semaphore_wait(barrier, len(friends) + jnp.minimum(block, REACH))

    sent = []

    def go(copy):
        copy.start()
        sent.append(copy)

    def same(ref, send, recv, device):
        return remote(ref, ref, send, recv, device)

    low, high = pl.ds(0, ROWS // 2), pl.ds(ROWS // 2, ROWS // 2)

    def y_copy(k):
        slot = OFFSETS.index(-k)
        return remote(g.at[core, 0, 0], g.at[core, 0, slot], y_send.at[slot - 1], y_recv.at[slot - 1],
                      at(x, along_y(k), core))

    def y_third(k):
        src, dst = OFFSETS.index(-2 * k), OFFSETS.index(-3 * k)
        return remote(g.at[core, 0, src], g.at[core, 0, dst], y_send.at[dst - 1], y_recv.at[dst - 1],
                      at(x, along_y(k), core))

    def y_fourth(k):
        rows, i = (low, 6) if k > 0 else (high, 7)
        return remote(g.at[core, 0, OFFSETS.index(-2 * k), rows], g.at[core, 0, 7, rows],
                      y_send.at[i], y_recv.at[i], at(x, along_y(2 * k), core))

    def x_copy(i, k):
        slots = pl.ds(GROUPS[i][0], GROUPS[i][1] - GROUPS[i][0])
        column = COLUMNS.index(2 if k == 2 else -k)
        n = 3 * i + column - 1
        return remote(g.at[core, 0, slots], g.at[core, column, slots], x_send.at[n], x_recv.at[n],
                      at(along_x(k), y, core))

    def row_copy(k):
        slot = OFFSETS.index(-k)
        columns = pl.ds(1, NX - 1)
        return remote(g.at[core, columns, 0], g.at[core, columns, slot], f_send.at[slot - 1], f_recv.at[slot - 1],
                      at(x, along_y(k), core))

    def sib(row, i, c):
        slots = pl.ds(GROUPS[i][0], GROUPS[i][1] - GROUPS[i][0])
        columns = pl.ds(1, NX - 1) if row else pl.ds(0, 1)
        ref = g.at[c, columns, slots]
        n = len(GROUPS) * row + i
        return remote(ref, ref, s_send.at[n], s_recv.at[n], sibling)

    def x_all(i):
        for k in (2, 1, -1):
            go(x_copy(i, k))

    x_all(0)
    for k in (2, -2, 1, -1):
        go(y_copy(k))
    for d in range(1, REACH + 1):
        if_earlier(d, lambda d=d: pl.semaphore_signal(
            z_ready.at[d - 1], inc=1, device_id={"ctx": block - d}, device_id_type=MESH))

    go(sib(0, 0, core))

    def dots(row, i):
        for c in range(1, NX) if row else (0,):
            for slot in range(*GROUPS[i]):
                chip = along_x(COLUMNS[c]) * NY + along_y(OFFSETS[slot])
                lhs = jnp.concatenate([g[0, c, slot], g[1, c, slot]], axis=1)
                rows = pl.ds(pl.multiple_of(chip * (2 * LOCAL), 2 * LOCAL), 2 * LOCAL)
                acc[...] += jnp.dot(lhs, w[rows, :], preferred_element_type=F32)
                f = lhs.astype(F32)
                f = f * f
                sq[...] += f[:, :LOCAL] + f[:, LOCAL:]

    def col0(i):
        if i == 1:
            y_copy(1).wait_recv()
            y_copy(-1).wait_recv()
        elif i == 2:
            for k in (1, -1):
                y_copy(2 * k).wait_recv()
                go(y_fourth(k))
                go(y_third(k))
        elif i == 3:
            y_third(1).wait_recv()
            y_third(-1).wait_recv()
        else:
            y_fourth(1).wait_recv()
            y_fourth(-1).wait_recv()
        if i != BY_Y:
            x_all(i)
        go(sib(0, i, core))

    def row(i):
        if i == BY_Y:
            row_copy(1).wait_recv()
            row_copy(-1).wait_recv()
        else:
            for k in (1, -1, 2):
                x_copy(i, k).wait_recv()
        if i == 0:
            go(row_copy(1))
            go(row_copy(-1))
        go(sib(1, i, core))

    def use(row, i):
        sib(row, i, 1 - core).wait_recv()
        dots(row, i)

    acc[...] = jnp.zeros_like(acc)
    sq[...] = jnp.zeros_like(sq)
    for p in params:
        p.wait()
    first_token = block * ROWS
    start, first_in, last_in, last_before = jnp.int32(0), jnp.int32(ROWS), jnp.int32(-1), jnp.int32(-1)
    starts = []
    for i in range(docs.shape[0]):
        here = start - first_token
        starts.append(here)
        inside = jnp.logical_and(here >= 0, here < ROWS)
        first_in = jnp.where(inside, jnp.minimum(first_in, here), first_in)
        last_in = jnp.where(inside, jnp.maximum(last_in, here), last_in)
        last_before = jnp.where(here < 0, jnp.maximum(last_before, start), last_before)
        start = start + docs[i]
    rate = pole[...]
    lam = jnp.exp(-rate)
    r2 = rate * rate
    series = 2.0 * jnp.exp(-rate) * rate * (
        1.0 + r2 * (1.0 / 6.0) * (1.0 + r2 * (1.0 / 20.0) * (1.0 + r2 * (1.0 / 42.0) * (1.0 + r2 * (1.0 / 72.0))))
    )
    mix = resid[...] * jnp.sqrt(jnp.where(rate < 0.5, series, 1.0 - jnp.exp(-2.0 * rate)))

    def end_weight(t, _):
        on = jnp.where(t >= last_in, 1.0, 0.0)
        sw[t] = jnp.exp(rate * (t - (ROWS - 1)).astype(F32)) * on
        return 0

    def from_before(t, _):
        on = jnp.where(t < first_in, 1.0, 0.0)
        t2[t] = mix * jnp.exp(rate * (-1 - t).astype(F32)) * on
        return 0

    def decay(t, _):
        is_start = functools.reduce(jnp.logical_or, [t == s for s in starts])
        lk[t] = lam * jnp.where(is_start, 0.0, 1.0)
        return 0

    lax.fori_loop(0, ROWS, end_weight, 0, unroll=8)
    col0(1)
    col0(2)
    row(0)
    lax.fori_loop(0, ROWS, from_before, 0, unroll=8)
    for p in parts:
        p.wait()
    use(0, 0)
    use(0, 1)
    col0(3)
    col0(4)
    use(1, 0)
    use(0, 2)
    row(2)
    row(1)
    use(0, 3)
    lax.fori_loop(0, ROWS, decay, 0, unroll=8)
    for d in range(1, REACH + 1):
        on = jnp.where(last_before < first_token - (d - 1) * ROWS, 1.0, 0.0)
        gains[d - 1] = jnp.exp(rate * (-(d - 1.0) * ROWS)) * on
    use(0, 4)
    use(1, 2)
    use(1, 1)
    row(3)
    row(4)
    use(1, 3)
    use(1, 4)

    rowscale = lax.rsqrt(jnp.sum(sq[...], axis=1, keepdims=True) / width + 1e-06)
    drv[...] = (acc[:, LOCAL:2 * LOCAL] * rowscale) * (acc[:, 2 * LOCAL:] * rowscale)

    def end_state(i, carry):
        even, odd = carry
        rows = drv[pl.ds(pl.multiple_of(i * 8, 8), 8), :]
        for r in range(0, 8, 2):
            even = even + sw[i * 8 + r] * rows[r:r + 1, :]
            odd = odd + sw[i * 8 + r + 1] * rows[r + 1:r + 2, :]
        return even, odd

    nought = jnp.zeros((MODES, LOCAL), F32)
    even, odd = lax.fori_loop(0, ROWS // 8, end_state, (nought, nought), unroll=2)
    mine[...] = even + odd
    zs = [
        remote(mine, got.at[d - 1], z_send.at[d - 1], z_recv.at[d - 1], {"ctx": block + d})
        for d in range(1, REACH + 1)
    ]
    for d in range(REACH, 0, -1):
        def to_later(d=d):
            pl.semaphore_wait(z_ready.at[d - 1], 1)
            zs[d - 1].start()
        if_later(d, to_later)

    def scan(i, state):
        rows = drv[pl.ds(pl.multiple_of(i * 8, 8), 8), :]
        for r in range(8):
            state = lk[i * 8 + r] * state + rows[r:r + 1, :]
            terms = mix * state
            y8[pl.ds(pl.multiple_of((i * 8 + r) * 8, 8), 8), :] = terms[:8] + terms[8:]
        return state

    lax.fori_loop(0, ROWS // 8, scan, nought)
    drv[...] = skip[...] * drv[...] + functools.reduce(
        jnp.add, [y8[pl.ds(s, ROWS, stride=8), :] for s in range(8)]
    )
    acc[:, :LOCAL] = acc[:, :LOCAL] * rowscale

    before = nought
    for d in range(1, REACH + 1):
        if_earlier(d, zs[d - 1].wait_recv)
        before = before + gains[d - 1] * got[d - 1]

    def carried(t, _):
        terms = t2[t] * before
        y8[pl.ds(pl.multiple_of(t * 8, 8), 8), :] = terms[:8] + terms[8:]
        return 0

    lax.fori_loop(0, ROWS, carried, 0, unroll=8)
    total = drv[...] + functools.reduce(
        jnp.add, [y8[pl.ds(s, ROWS, stride=8), :] for s in range(8)]
    )
    out[...] = (acc[:, :LOCAL] * total).astype(out.dtype)

    for c in sent:
        c.wait_send()
    for d in range(1, REACH + 1):
        if_later(d, zs[d - 1].wait_send)


def per_device(n_ctx, stream, in_weight, pole_rate, residue, skip_gain, doc_lengths):
    width = in_weight.shape[0]
    hbm = pl.BlockSpec(memory_space=pltpu.MemorySpace.HBM)
    dma = pltpu.SemaphoreType.DMA
    vmem = pltpu.VMEM
    bf16 = jnp.bfloat16
    return pl.pallas_call(
        functools.partial(kernel, n_ctx, width),
        out_shape=jax.ShapeDtypeStruct((ROWS, LOCAL), bf16),
        in_specs=[hbm] * 6,
        out_specs=pl.BlockSpec(memory_space=pltpu.VMEM),
        scratch_shapes=[
            vmem((2, NX, NY, ROWS, LOCAL), bf16),
            vmem((width, 3 * LOCAL), bf16),
            vmem((ROWS, 3 * LOCAL), F32),
            vmem((ROWS, LOCAL), F32),
            vmem((ROWS, LOCAL), F32),
            vmem((ROWS * 8, LOCAL), F32),
            vmem((ROWS, MODES, LOCAL), F32),
            vmem((ROWS, MODES, LOCAL), F32),
            vmem((ROWS, MODES, LOCAL), F32),
            vmem((MODES, LOCAL), F32),
            vmem((MODES, LOCAL), F32),
            vmem((1, LOCAL), F32),
            vmem((MODES, LOCAL), F32),
            vmem((REACH, MODES, LOCAL), F32),
            vmem((REACH, MODES, LOCAL), F32),
            pltpu.SMEM((doc_lengths.shape[0],), jnp.int32),
            dma((3,)), dma((4,)), dma,
            dma((NY,)), dma((NY,)),
            dma((3 * len(GROUPS),)), dma((3 * len(GROUPS),)), dma((2,)), dma((2,)),
            dma((2 * len(GROUPS),)), dma((2 * len(GROUPS),)),
            dma((REACH,)), dma((REACH,)), pltpu.SemaphoreType.REGULAR((REACH,)),
        ],
        compiler_params=pltpu.CompilerParams(
            collective_id=0, has_side_effects=True, vmem_limit_bytes=60 << 20
        ),
        name="hyena",
    )(
        stream, jnp.transpose(in_weight, (1, 0, 2)), pole_rate.T, residue.T,
        skip_gain.reshape(1, LOCAL), doc_lengths,
    )


def solution(mesh):
    placed = (P("ctx", "ch"), P(None, None, "ch"), P("ch", None), P("ch", None), P("ch"), P())
    return jax.shard_map(
        functools.partial(per_device, mesh.shape["ctx"]),
        mesh=mesh, in_specs=placed, out_specs=P("ctx", "ch"), check_vma=False,
    )
```

```python
import functools

import jax
import jax.numpy as jnp
from jax import lax
from jax.experimental import pallas as pl
from jax.experimental.pallas import tpu as pltpu
from jax.sharding import PartitionSpec as P

MESH = pl.DeviceIdType.MESH
NX, NY = 4, 8
ROWS = 128
LOCAL = 128
MODES = 16
OFFSETS = (0, 1, -1, 2, -2, 3, -3, 4)
GROUPS = ((0, 1), (1, 3), (3, 5), (5, 7), (7, 8))
BY_Y = 1
COLUMNS = (0, 1, -1, 2)
REACH = 6
F32 = jnp.float32


def kernel(
    n_ctx, width,
    stream, w3, pole_h, resid_h, skip_h, docs_h, out,
    g, w, acc, sq, drv, y8, sw, lk, t2, mixes, pole, resid, skip, mine, got, gains, docs,
    w_sem, prm_sem, own_sem,
    y_send, y_recv, x_send, x_recv, f_send, f_recv, s_send, s_recv,
    z_send, z_recv, z_ready,
):
    block = lax.axis_index("ctx")
    ch = lax.axis_index("ch")
    core = lax.rem(ch, 2)
    y = lax.rem(ch // 2, NY)
    x = ch // (2 * NY)

    def at(px, py, pc):
        return {"ch": (px * NY + py) * 2 + pc}

    def along_x(k):
        return lax.rem(x + (k + NX), NX)

    def along_y(k):
        return lax.rem(y + (k + NY), NY)

    def remote(src, dst, send, recv, device):
        return pltpu.make_async_remote_copy(
            src_ref=src, dst_ref=dst, send_sem=send, recv_sem=recv,
            device_id=device, device_id_type=MESH,
        )

    parts = [
        pltpu.make_async_copy(w3.at[j], w.at[:, pl.ds(j * LOCAL, LOCAL)], w_sem.at[j])
        for j in range(3)
    ]
    params = [
        pltpu.make_async_copy(src, dst, prm_sem.at[i])
        for i, (src, dst) in enumerate(
            ((pole_h, pole), (resid_h, resid), (skip_h, skip), (docs_h, docs))
        )
    ]
    own = pltpu.make_async_copy(stream, g.at[core, 0, 0], own_sem)
    own.start()
    for p in params:
        p.start()

    sibling = at(x, y, 1 - core)
    friends = [sibling]
    friends += [at(along_x(k), y, core) for k in (1, -1, 2)]
    friends += [at(x, along_y(k), core) for k in range(1, NY)]
    barrier = pltpu.get_barrier_semaphore()
    for friend in friends:
        pl.semaphore_signal(barrier, inc=1, device_id=friend, device_id_type=MESH)

    def if_later(d, action):
        pl.when(block + d < n_ctx)(action)

    def if_earlier(d, action):
        pl.when(block >= d)(action)

    for d in range(1, REACH + 1):
        if_later(d, lambda d=d: pl.semaphore_signal(
            barrier, inc=1, device_id={"ctx": block + d}, device_id_type=MESH))
    own.wait()
    for p in parts:
        p.start()
    got[...] = jnp.zeros_like(got)
    pl.semaphore_wait(barrier, len(friends) + jnp.minimum(block, REACH))

    sent = []

    def go(copy):
        copy.start()
        sent.append(copy)

    def same(ref, send, recv, device):
        return remote(ref, ref, send, recv, device)

    low, high = pl.ds(0, ROWS // 2), pl.ds(ROWS // 2, ROWS // 2)

    def y_copy(k):
        slot = OFFSETS.index(4 if k == 4 else -k)
        return remote(g.at[core, 0, 0], g.at[core, 0, slot], y_send.at[slot - 1], y_recv.at[slot - 1],
                      at(x, along_y(k), core))

    def x_copy(i, k):
        slots = pl.ds(GROUPS[i][0], GROUPS[i][1] - GROUPS[i][0])
        column = COLUMNS.index(2 if k == 2 else -k)
        n = 3 * i + column - 1
        return remote(g.at[core, 0, slots], g.at[core, column, slots], x_send.at[n], x_recv.at[n],
                      at(along_x(k), y, core))

    def row_copy(k):
        slot = OFFSETS.index(-k)
        columns = pl.ds(1, NX - 1)
        return remote(g.at[core, columns, 0], g.at[core, columns, slot], f_send.at[slot - 1], f_recv.at[slot - 1],
                      at(x, along_y(k), core))

    def sib(row, i, c):
        slots = pl.ds(GROUPS[i][0], GROUPS[i][1] - GROUPS[i][0])
        columns = pl.ds(1, NX - 1) if row else pl.ds(0, 1)
        ref = g.at[c, columns, slots]
        n = len(GROUPS) * row + i
        return remote(ref, ref, s_send.at[n], s_recv.at[n], sibling)

    def x_all(i):
        for k in (2, 1, -1):
            go(x_copy(i, k))

    x_all(0)
    for k in (1, -1, 2, -2, 3, -3, 4):
        go(y_copy(k))
    for d in range(1, REACH + 1):
        if_earlier(d, lambda d=d: pl.semaphore_signal(
            z_ready.at[d - 1], inc=1, device_id={"ctx": block - d}, device_id_type=MESH))

    go(sib(0, 0, core))

    def dots(row, i):
        for c in range(1, NX) if row else (0,):
            for slot in range(*GROUPS[i]):
                chip = along_x(COLUMNS[c]) * NY + along_y(OFFSETS[slot])
                lhs = jnp.concatenate([g[0, c, slot], g[1, c, slot]], axis=1)
                rows = pl.ds(pl.multiple_of(chip * (2 * LOCAL), 2 * LOCAL), 2 * LOCAL)
                acc[...] += jnp.dot(lhs, w[rows, :], preferred_element_type=F32)
                f = lhs.astype(F32)
                f = f * f
                sq[...] += f[:, :LOCAL] + f[:, LOCAL:]

    def col0(i):
        for slot in range(*GROUPS[i]):
            k = OFFSETS[slot]
            y_copy(4 if k == 4 else -k).wait_recv()
        if i != BY_Y:
            x_all(i)
        go(sib(0, i, core))

    def row(i):
        if i == BY_Y:
            row_copy(1).wait_recv()
            row_copy(-1).wait_recv()
        else:
            for k in (1, -1, 2):
                x_copy(i, k).wait_recv()
        if i == 0:
            go(row_copy(1))
            go(row_copy(-1))
        go(sib(1, i, core))

    def use(row, i):
        sib(row, i, 1 - core).wait_recv()
        dots(row, i)

    acc[...] = jnp.zeros_like(acc)
    sq[...] = jnp.zeros_like(sq)
    for p in params:
        p.wait()
    first_token = block * ROWS
    start, first_in, last_in, last_before = jnp.int32(0), jnp.int32(ROWS), jnp.int32(-1), jnp.int32(-1)
    starts = []
    for i in range(docs.shape[0]):
        here = start - first_token
        starts.append(here)
        inside = jnp.logical_and(here >= 0, here < ROWS)
        first_in = jnp.where(inside, jnp.minimum(first_in, here), first_in)
        last_in = jnp.where(inside, jnp.maximum(last_in, here), last_in)
        last_before = jnp.where(here < 0, jnp.maximum(last_before, start), last_before)
        start = start + docs[i]
    rate = pole[...]
    lam = jnp.exp(-rate)
    r2 = rate * rate
    series = 2.0 * jnp.exp(-rate) * rate * (
        1.0 + r2 * (1.0 / 6.0) * (1.0 + r2 * (1.0 / 20.0) * (1.0 + r2 * (1.0 / 42.0) * (1.0 + r2 * (1.0 / 72.0))))
    )
    mix = resid[...] * jnp.sqrt(jnp.where(rate < 0.5, series, 1.0 - jnp.exp(-2.0 * rate)))

    def end_weight(t, _):
        on = jnp.where(t >= last_in, 1.0, 0.0)
        sw[t] = jnp.exp(rate * (t - (ROWS - 1)).astype(F32)) * on
        return 0

    mixes[...] = mix
    token = lax.broadcasted_iota(jnp.int32, (ROWS, LOCAL), 0)
    ages = (-1 - token).astype(F32)
    on_before = jnp.where(token < first_in, 1.0, 0.0)

    def from_before(n, _):
        t2[n] = mixes[pl.ds(n, 1), :] * jnp.exp(pole[pl.ds(n, 1), :] * ages) * on_before
        return 0

    def decay(t, _):
        is_start = functools.reduce(jnp.logical_or, [t == s for s in starts])
        lk[t] = lam * jnp.where(is_start, 0.0, 1.0)
        return 0

    lax.fori_loop(0, ROWS, end_weight, 0, unroll=8)
    col0(1)
    col0(2)
    row(0)
    lax.fori_loop(0, MODES, from_before, 0)
    for p in parts:
        p.wait()
    use(0, 0)
    use(0, 1)
    col0(3)
    col0(4)
    use(1, 0)
    use(0, 2)
    row(2)
    row(1)
    use(0, 3)
    lax.fori_loop(0, ROWS, decay, 0, unroll=8)
    for d in range(1, REACH + 1):
        on = jnp.where(last_before < first_token - (d - 1) * ROWS, 1.0, 0.0)
        gains[d - 1] = jnp.exp(rate * (-(d - 1.0) * ROWS)) * on
    use(0, 4)
    use(1, 2)
    use(1, 1)
    row(3)
    row(4)
    use(1, 3)
    use(1, 4)

    rowscale = lax.rsqrt(jnp.sum(sq[...], axis=1, keepdims=True) / width + 1e-06)
    drv[...] = (acc[:, LOCAL:2 * LOCAL] * rowscale) * (acc[:, 2 * LOCAL:] * rowscale)

    def end_state(i, carry):
        even, odd = carry
        rows = drv[pl.ds(pl.multiple_of(i * 8, 8), 8), :]
        for r in range(0, 8, 2):
            even = even + sw[i * 8 + r] * rows[r:r + 1, :]
            odd = odd + sw[i * 8 + r + 1] * rows[r + 1:r + 2, :]
        return even, odd

    nought = jnp.zeros((MODES, LOCAL), F32)
    even, odd = lax.fori_loop(0, ROWS // 8, end_state, (nought, nought), unroll=2)
    mine[...] = even + odd
    zs = [
        remote(mine, got.at[d - 1], z_send.at[d - 1], z_recv.at[d - 1], {"ctx": block + d})
        for d in range(1, REACH + 1)
    ]
    for d in range(REACH, 0, -1):
        def to_later(d=d):
            pl.semaphore_wait(z_ready.at[d - 1], 1)
            zs[d - 1].start()
        if_later(d, to_later)

    def scan(i, state):
        rows = drv[pl.ds(pl.multiple_of(i * 8, 8), 8), :]
        for r in range(8):
            state = lk[i * 8 + r] * state + rows[r:r + 1, :]
            terms = mix * state
            y8[pl.ds(pl.multiple_of((i * 8 + r) * 8, 8), 8), :] = terms[:8] + terms[8:]
        return state

    lax.fori_loop(0, ROWS // 8, scan, nought)
    drv[...] = skip[...] * drv[...] + functools.reduce(
        jnp.add, [y8[pl.ds(s, ROWS, stride=8), :] for s in range(8)]
    )
    acc[:, :LOCAL] = acc[:, :LOCAL] * rowscale

    before = nought
    for d in range(1, REACH + 1):
        if_earlier(d, zs[d - 1].wait_recv)
        before = before + gains[d - 1] * got[d - 1]

    total = drv[...]
    for n in range(MODES):
        total = total + t2[n] * before[n:n + 1, :]
    out[...] = (acc[:, :LOCAL] * total).astype(out.dtype)

    for c in sent:
        c.wait_send()
    for d in range(1, REACH + 1):
        if_later(d, zs[d - 1].wait_send)


def per_device(n_ctx, stream, in_weight, pole_rate, residue, skip_gain, doc_lengths):
    width = in_weight.shape[0]
    hbm = pl.BlockSpec(memory_space=pltpu.MemorySpace.HBM)
    dma = pltpu.SemaphoreType.DMA
    vmem = pltpu.VMEM
    bf16 = jnp.bfloat16
    return pl.pallas_call(
        functools.partial(kernel, n_ctx, width),
        out_shape=jax.ShapeDtypeStruct((ROWS, LOCAL), bf16),
        in_specs=[hbm] * 6,
        out_specs=pl.BlockSpec(memory_space=pltpu.VMEM),
        scratch_shapes=[
            vmem((2, NX, NY, ROWS, LOCAL), bf16),
            vmem((width, 3 * LOCAL), bf16),
            vmem((ROWS, 3 * LOCAL), F32),
            vmem((ROWS, LOCAL), F32),
            vmem((ROWS, LOCAL), F32),
            vmem((ROWS * 8, LOCAL), F32),
            vmem((ROWS, MODES, LOCAL), F32),
            vmem((ROWS, MODES, LOCAL), F32),
            vmem((MODES, ROWS, LOCAL), F32),
            vmem((MODES, LOCAL), F32),
            vmem((MODES, LOCAL), F32),
            vmem((MODES, LOCAL), F32),
            vmem((1, LOCAL), F32),
            vmem((MODES, LOCAL), F32),
            vmem((REACH, MODES, LOCAL), F32),
            vmem((REACH, MODES, LOCAL), F32),
            pltpu.SMEM((doc_lengths.shape[0],), jnp.int32),
            dma((3,)), dma((4,)), dma,
            dma((NY,)), dma((NY,)),
            dma((3 * len(GROUPS),)), dma((3 * len(GROUPS),)), dma((2,)), dma((2,)),
            dma((2 * len(GROUPS),)), dma((2 * len(GROUPS),)),
            dma((REACH,)), dma((REACH,)), pltpu.SemaphoreType.REGULAR((REACH,)),
        ],
        compiler_params=pltpu.CompilerParams(
            collective_id=0, has_side_effects=True, vmem_limit_bytes=60 << 20
        ),
        name="hyena",
    )(
        stream, jnp.transpose(in_weight, (1, 0, 2)), pole_rate.T, residue.T,
        skip_gain.reshape(1, LOCAL), doc_lengths,
    )


def solution(mesh):
    placed = (P("ctx", "ch"), P(None, None, "ch"), P("ch", None), P("ch", None), P("ch"), P())
    return jax.shard_map(
        functools.partial(per_device, mesh.shape["ctx"]),
        mesh=mesh, in_specs=placed, out_specs=P("ctx", "ch"), check_vma=False,
    )
```

```python
import functools

import jax
import jax.numpy as jnp
from jax import lax
from jax.experimental import pallas as pl
from jax.experimental.pallas import tpu as pltpu
from jax.sharding import PartitionSpec as P

MESH = pl.DeviceIdType.MESH
NX, NY = 4, 8
ROWS = 128
LOCAL = 128
MODES = 16
OFFSETS = (0, 1, -1, 2, -2, 3, -3, 4)
GROUPS = ((0, 1), (1, 3), (3, 5), (5, 7), (7, 8))
BY_Y = 1
COLUMNS = (0, 1, -1, 2)
REACH = 6
F32 = jnp.float32


def kernel(
    n_ctx, width,
    stream, w3, pole_h, resid_h, skip_h, docs_h, out,
    g, w, acc, sq, drv, y8, sw, lk, t2, t3, mixes, pole, resid, skip, mine, got, gains, docs,
    w_sem, prm_sem, own_sem,
    y_send, y_recv, x_send, x_recv, f_send, f_recv, s_send, s_recv,
    z_send, z_recv, z_ready,
):
    block = lax.axis_index("ctx")
    ch = lax.axis_index("ch")
    core = lax.rem(ch, 2)
    y = lax.rem(ch // 2, NY)
    x = ch // (2 * NY)

    def at(px, py, pc):
        return {"ch": (px * NY + py) * 2 + pc}

    def along_x(k):
        return lax.rem(x + (k + NX), NX)

    def along_y(k):
        return lax.rem(y + (k + NY), NY)

    def remote(src, dst, send, recv, device):
        return pltpu.make_async_remote_copy(
            src_ref=src, dst_ref=dst, send_sem=send, recv_sem=recv,
            device_id=device, device_id_type=MESH,
        )

    parts = [
        pltpu.make_async_copy(w3.at[j], w.at[:, pl.ds(j * LOCAL, LOCAL)], w_sem.at[j])
        for j in range(3)
    ]
    params = [
        pltpu.make_async_copy(src, dst, prm_sem.at[i])
        for i, (src, dst) in enumerate(
            ((pole_h, pole), (resid_h, resid), (skip_h, skip), (docs_h, docs))
        )
    ]
    own = pltpu.make_async_copy(stream, g.at[core, 0, 0], own_sem)
    own.start()
    for p in params:
        p.start()

    sibling = at(x, y, 1 - core)
    friends = [sibling]
    friends += [at(along_x(k), y, core) for k in (1, -1, 2)]
    friends += [at(x, along_y(k), core) for k in range(1, NY)]
    barrier = pltpu.get_barrier_semaphore()
    for friend in friends:
        pl.semaphore_signal(barrier, inc=1, device_id=friend, device_id_type=MESH)

    def if_later(d, action):
        pl.when(block + d < n_ctx)(action)

    def if_earlier(d, action):
        pl.when(block >= d)(action)

    for d in range(1, REACH + 1):
        if_later(d, lambda d=d: pl.semaphore_signal(
            barrier, inc=1, device_id={"ctx": block + d}, device_id_type=MESH))
    own.wait()
    for p in parts:
        p.start()
    got[...] = jnp.zeros_like(got)
    pl.semaphore_wait(barrier, len(friends) + jnp.minimum(block, REACH))

    sent = []

    def go(copy):
        copy.start()
        sent.append(copy)

    def same(ref, send, recv, device):
        return remote(ref, ref, send, recv, device)

    low, high = pl.ds(0, ROWS // 2), pl.ds(ROWS // 2, ROWS // 2)

    def y_copy(k):
        slot = OFFSETS.index(4 if k == 4 else -k)
        return remote(g.at[core, 0, 0], g.at[core, 0, slot], y_send.at[slot - 1], y_recv.at[slot - 1],
                      at(x, along_y(k), core))

    def x_copy(i, k):
        slots = pl.ds(GROUPS[i][0], GROUPS[i][1] - GROUPS[i][0])
        column = COLUMNS.index(2 if k == 2 else -k)
        n = 3 * i + column - 1
        return remote(g.at[core, 0, slots], g.at[core, column, slots], x_send.at[n], x_recv.at[n],
                      at(along_x(k), y, core))

    def row_copy(k):
        slot = OFFSETS.index(-k)
        columns = pl.ds(1, NX - 1)
        return remote(g.at[core, columns, 0], g.at[core, columns, slot], f_send.at[slot - 1], f_recv.at[slot - 1],
                      at(x, along_y(k), core))

    def sib(row, i, c):
        slots = pl.ds(GROUPS[i][0], GROUPS[i][1] - GROUPS[i][0])
        columns = pl.ds(1, NX - 1) if row else pl.ds(0, 1)
        ref = g.at[c, columns, slots]
        n = len(GROUPS) * row + i
        return remote(ref, ref, s_send.at[n], s_recv.at[n], sibling)

    def x_all(i):
        for k in (2, 1, -1):
            go(x_copy(i, k))

    for k in (1, -1, 2, -2, 3, -3, 4):
        go(y_copy(k))
    x_all(0)
    for d in range(1, REACH + 1):
        if_earlier(d, lambda d=d: pl.semaphore_signal(
            z_ready.at[d - 1], inc=1, device_id={"ctx": block - d}, device_id_type=MESH))

    go(sib(0, 0, core))

    def dots(row, i):
        total = squares = None
        for c in range(1, NX) if row else (0,):
            for slot in range(*GROUPS[i]):
                chip = along_x(COLUMNS[c]) * NY + along_y(OFFSETS[slot])
                lhs = jnp.concatenate([g[0, c, slot], g[1, c, slot]], axis=1)
                rows = pl.ds(pl.multiple_of(chip * (2 * LOCAL), 2 * LOCAL), 2 * LOCAL)
                product = jnp.dot(lhs, w[rows, :], preferred_element_type=F32)
                total = product if total is None else total + product
                f = lhs.astype(F32)
                f = f * f
                f = f[:, :LOCAL] + f[:, LOCAL:]
                squares = f if squares is None else squares + f
        acc[...] += total
        sq[...] += squares

    def col0(i):
        for slot in range(*GROUPS[i]):
            k = OFFSETS[slot]
            y_copy(4 if k == 4 else -k).wait_recv()
        if i != BY_Y:
            x_all(i)
        go(sib(0, i, core))

    def row(i):
        if i == BY_Y:
            row_copy(1).wait_recv()
            row_copy(-1).wait_recv()
        else:
            for k in (1, -1, 2):
                x_copy(i, k).wait_recv()
        if i == 0:
            go(row_copy(1))
            go(row_copy(-1))
        go(sib(1, i, core))

    def use(row, i):
        sib(row, i, 1 - core).wait_recv()
        dots(row, i)

    acc[...] = jnp.zeros_like(acc)
    sq[...] = jnp.zeros_like(sq)
    for p in params:
        p.wait()
    first_token = block * ROWS
    start, first_in, last_in, last_before = jnp.int32(0), jnp.int32(ROWS), jnp.int32(-1), jnp.int32(-1)
    starts, first_second = [], jnp.int32(ROWS)
    for i in range(docs.shape[0]):
        here = start - first_token
        starts.append(here)
        inside = jnp.logical_and(here >= 0, here < ROWS)
        late = jnp.logical_and(here >= ROWS // 2, here < ROWS)
        first_second = jnp.where(late, jnp.minimum(first_second, here), first_second)
        first_in = jnp.where(inside, jnp.minimum(first_in, here), first_in)
        last_in = jnp.where(inside, jnp.maximum(last_in, here), last_in)
        last_before = jnp.where(here < 0, jnp.maximum(last_before, start), last_before)
        start = start + docs[i]
    rate = pole[...]
    lam = jnp.exp(-rate)
    r2 = rate * rate
    series = 2.0 * jnp.exp(-rate) * rate * (
        1.0 + r2 * (1.0 / 6.0) * (1.0 + r2 * (1.0 / 20.0) * (1.0 + r2 * (1.0 / 42.0) * (1.0 + r2 * (1.0 / 72.0))))
    )
    mix = resid[...] * jnp.sqrt(jnp.where(rate < 0.5, series, 1.0 - jnp.exp(-2.0 * rate)))

    def end_weight(t, _):
        on = jnp.where(t >= last_in, 1.0, 0.0)
        sw[t] = jnp.exp(rate * (t - (ROWS - 1)).astype(F32)) * on
        return 0

    mixes[...] = mix
    token = lax.broadcasted_iota(jnp.int32, (ROWS, LOCAL), 0)
    ages = (-1 - token).astype(F32)
    on_before = jnp.where(token < first_in, 1.0, 0.0)

    def from_before(n, _):
        t2[n] = mixes[pl.ds(n, 1), :] * jnp.exp(pole[pl.ds(n, 1), :] * ages) * on_before
        return 0

    second = lax.broadcasted_iota(jnp.int32, (ROWS // 2, LOCAL), 0)
    second_ages = (-1 - second).astype(F32)
    on_second = jnp.where(second + ROWS // 2 < first_second, 1.0, 0.0)

    def from_first(n, _):
        t3[n] = mixes[pl.ds(n, 1), :] * jnp.exp(pole[pl.ds(n, 1), :] * second_ages) * on_second
        return 0

    def decay(t, _):
        is_start = functools.reduce(jnp.logical_or, [t == s for s in starts])
        lk[t] = lam * jnp.where(is_start, 0.0, 1.0)
        return 0

    lax.fori_loop(0, ROWS, end_weight, 0, unroll=8)
    col0(1)
    col0(2)
    row(0)
    lax.fori_loop(0, MODES, from_before, 0)
    for p in parts:
        p.wait()
    use(0, 0)
    use(0, 1)
    col0(3)
    col0(4)
    use(1, 0)
    use(0, 2)
    row(2)
    row(1)
    use(0, 3)
    lax.fori_loop(0, ROWS, decay, 0, unroll=8)
    lax.fori_loop(0, MODES, from_first, 0)
    for d in range(1, REACH + 1):
        on = jnp.where(last_before < first_token - (d - 1) * ROWS, 1.0, 0.0)
        gains[d - 1] = jnp.exp(rate * (-(d - 1.0) * ROWS)) * on
    use(0, 4)
    use(1, 2)
    use(1, 1)
    row(3)
    row(4)
    use(1, 3)
    use(1, 4)

    rowscale = lax.rsqrt(jnp.sum(sq[...], axis=1, keepdims=True) / width + 1e-06)
    drv[...] = (acc[:, LOCAL:2 * LOCAL] * rowscale) * (acc[:, 2 * LOCAL:] * rowscale)

    def end_state(i, carry):
        even, odd = carry
        rows = drv[pl.ds(pl.multiple_of(i * 8, 8), 8), :]
        for r in range(0, 8, 2):
            even = even + sw[i * 8 + r] * rows[r:r + 1, :]
            odd = odd + sw[i * 8 + r + 1] * rows[r + 1:r + 2, :]
        return even, odd

    nought = jnp.zeros((MODES, LOCAL), F32)
    even, odd = lax.fori_loop(0, ROWS // 8, end_state, (nought, nought), unroll=2)
    mine[...] = even + odd
    zs = [
        remote(mine, got.at[d - 1], z_send.at[d - 1], z_recv.at[d - 1], {"ctx": block + d})
        for d in range(1, REACH + 1)
    ]
    for d in range(REACH, 0, -1):
        def to_later(d=d):
            pl.semaphore_wait(z_ready.at[d - 1], 1)
            zs[d - 1].start()
        if_later(d, to_later)

    half = ROWS // 2

    def scan(i, states):
        states = list(states)
        rows = [drv[pl.ds(pl.multiple_of(h * half + i * 8, 8), 8), :] for h in range(2)]
        for r in range(8):
            for h in range(2):
                t = h * half + i * 8 + r
                states[h] = lk[t] * states[h] + rows[h][r:r + 1, :]
                terms = mix * states[h]
                y8[pl.ds(pl.multiple_of(t * 8, 8), 8), :] = terms[:8] + terms[8:]
        return tuple(states)

    middle, _ = lax.fori_loop(0, half // 8, scan, (nought, nought))
    drv[...] = skip[...] * drv[...] + functools.reduce(
        jnp.add, [y8[pl.ds(s, ROWS, stride=8), :] for s in range(8)]
    )
    carried = drv[half:, :]
    for n in range(MODES):
        carried = carried + t3[n] * middle[n:n + 1, :]
    drv[half:, :] = carried
    acc[:, :LOCAL] = acc[:, :LOCAL] * rowscale

    before = nought
    for d in range(1, REACH + 1):
        if_earlier(d, zs[d - 1].wait_recv)
        before = before + gains[d - 1] * got[d - 1]

    total = drv[...]
    for n in range(MODES):
        total = total + t2[n] * before[n:n + 1, :]
    out[...] = (acc[:, :LOCAL] * total).astype(out.dtype)

    for c in sent:
        c.wait_send()
    for d in range(1, REACH + 1):
        if_later(d, zs[d - 1].wait_send)


def per_device(n_ctx, stream, in_weight, pole_rate, residue, skip_gain, doc_lengths):
    width = in_weight.shape[0]
    hbm = pl.BlockSpec(memory_space=pltpu.MemorySpace.HBM)
    dma = pltpu.SemaphoreType.DMA
    vmem = pltpu.VMEM
    bf16 = jnp.bfloat16
    return pl.pallas_call(
        functools.partial(kernel, n_ctx, width),
        out_shape=jax.ShapeDtypeStruct((ROWS, LOCAL), bf16),
        in_specs=[hbm] * 6,
        out_specs=pl.BlockSpec(memory_space=pltpu.VMEM),
        scratch_shapes=[
            vmem((2, NX, NY, ROWS, LOCAL), bf16),
            vmem((width, 3 * LOCAL), bf16),
            vmem((ROWS, 3 * LOCAL), F32),
            vmem((ROWS, LOCAL), F32),
            vmem((ROWS, LOCAL), F32),
            vmem((ROWS * 8, LOCAL), F32),
            vmem((ROWS, MODES, LOCAL), F32),
            vmem((ROWS, MODES, LOCAL), F32),
            vmem((MODES, ROWS, LOCAL), F32),
            vmem((MODES, ROWS // 2, LOCAL), F32),
            vmem((MODES, LOCAL), F32),
            vmem((MODES, LOCAL), F32),
            vmem((MODES, LOCAL), F32),
            vmem((1, LOCAL), F32),
            vmem((MODES, LOCAL), F32),
            vmem((REACH, MODES, LOCAL), F32),
            vmem((REACH, MODES, LOCAL), F32),
            pltpu.SMEM((doc_lengths.shape[0],), jnp.int32),
            dma((3,)), dma((4,)), dma,
            dma((NY,)), dma((NY,)),
            dma((3 * len(GROUPS),)), dma((3 * len(GROUPS),)), dma((2,)), dma((2,)),
            dma((2 * len(GROUPS),)), dma((2 * len(GROUPS),)),
            dma((REACH,)), dma((REACH,)), pltpu.SemaphoreType.REGULAR((REACH,)),
        ],
        compiler_params=pltpu.CompilerParams(
            collective_id=0, has_side_effects=True, vmem_limit_bytes=60 << 20
        ),
        name="hyena",
    )(
        stream, jnp.transpose(in_weight, (1, 0, 2)), pole_rate.T, residue.T,
        skip_gain.reshape(1, LOCAL), doc_lengths,
    )


def solution(mesh):
    placed = (P("ctx", "ch"), P(None, None, "ch"), P("ch", None), P("ch", None), P("ch"), P())
    return jax.shard_map(
        functools.partial(per_device, mesh.shape["ctx"]),
        mesh=mesh, in_specs=placed, out_specs=P("ctx", "ch"), check_vma=False,
    )
```
